512 devices in a mesh: dp: 64 (over z, x), seq: 8 (over y, core).
Axes of the slice: x: 4, y: 4, z: 16, core: 2. Of those that a mesh axis runs over, the one named last changes fastest.
Arguments:
- acts: bfloat16 [65536, 4096], P('dp', 'seq'), may hold values from -6 to 6
- upstream: bfloat16 [65536, 1024], P(('dp', 'seq')), may hold values from -0.005859375 to 0.005859375
- keep_lists: int32 [64, 8], replicated, may hold values from 0 to 15, all different within a row
- left_gram: float32 [8, 64, 1, 64, 64], P('seq', 'dp'), as said below
- right_gram: float32 [8, 64, 1, 64, 64], P('seq', 'dp'), as said below
- left_basis: float32 [8, 64, 1, 64, 64], P('seq', 'dp'), may hold values from -0.75 to 0.75
- right_basis: float32 [8, 64, 1, 64, 64], P('seq', 'dp'), may hold values from -0.75 to 0.75
- second_moment: float32 [8, 64, 1, 64, 64], P('seq', 'dp'), may hold values from 0.004 to 0.04
Outputs:
- new_left: float32 [8, 64, 1, 64, 64], P('seq', 'dp')
- new_right: float32 [8, 64, 1, 64, 64], P('seq', 'dp')
- direction: float32 [8, 64, 1, 64, 64], P('seq', 'dp')
The draws below stay inside these ranges and needn't reach their ends.
Inputs may be any that keep to these rules, and one draw needn't show every extreme that they name: `keep_lists`: each row lists 8 different column blocks, and every column block is kept in some row. `left_gram`: each block is symmetric. `right_gram`: each block is symmetric.
All inputs are finite; a program needn't handle non-finite values.
Results may differ from the reference program's by a relative error of at most 0.0003.
Values may be sent and summed in bfloat16 or wider, within the bound.
No kernel may reach another device: no remote copies, remote signals or barrier semaphores. Data moves between devices by JAX's collectives and lax.ppermute only.
A program may use at most 64 MiB of HBM per device.

```python
import math
import jax
import jax.numpy as jnp
from jax import lax

D = 4096
K_COLS = 1024
BLOCK = 64
ROW_BLOCKS = 64
COL_BLOCKS = 16
KEPT = 8
OWNED = 1
TOKENS = 65536
DP_SHARDS = 64
SEQ_SHARDS = 8


def gram_draw(key):
    noise = jax.random.normal(key, (SEQ_SHARDS, DP_SHARDS, OWNED, BLOCK, BLOCK), jnp.float32) * 0.2
    symmetric = 0.5 * (noise + jnp.swapaxes(noise, -1, -2))
    return symmetric + 0.5 * jnp.eye(BLOCK, dtype=jnp.float32)


def draw_left_gram(key, part):
    return gram_draw(jax.random.fold_in(key, 11))


def draw_right_gram(key, part):
    return gram_draw(jax.random.fold_in(key, 23))


def levels(rng, dims, split, low, largest):
    gain = 1.0
    for position, parts in split:
        heights = jax.random.uniform(jax.random.fold_in(jax.random.fold_in(rng, 6), position), (parts,), jnp.float32, low / len(split), largest / len(split))
        gain = gain * jnp.repeat(jnp.exp(heights), dims[position] // parts).reshape((-1,) + (1,) * (len(dims) - 1 - position))
    return gain


def picks_of(own_key, rows, count, top, lift):
    sequence = jax.random.permutation(jax.random.fold_in(own_key, 1), count)
    pull = sequence
    for power in range(3):
        pull = pull * pull // count
    pull = pull * lift // count
    tickets = jax.random.randint(jax.random.fold_in(own_key, 2), (rows, count), 0, 4096) + pull
    holders = jax.random.permutation(jax.random.fold_in(own_key, 3), rows)[jnp.arange(count) % rows]
    tickets = jnp.where(jnp.arange(rows)[:, None] == holders[None, :], 1 << 14, tickets)
    score = tickets * count + jnp.arange(count)
    return lax.top_k(score.astype(jnp.int32), top)[1].astype(jnp.int32)


def gaussian(key, dims, width, limit, split=(), kind=jnp.bfloat16):
    result = width * jax.random.normal(key, dims, jnp.float32)
    if split:
        result = result * levels(key, dims, split, -0.22, 0.18)
    return jnp.clip(result, -limit, limit).astype(kind)


def setup_inputs(seed: int = 0) -> dict:
    key_list = jax.random.split(jax.random.key(seed), 9)
    acts = gaussian(key_list[0], (TOKENS, D), 1.0, 6.0, ((0, 64), (1, 8)))
    upstream = gaussian(key_list[1], (TOKENS, K_COLS), (0.25 * TOKENS ** -0.5), 0.005859375, ((0, 512),))
    keep_lists = picks_of(key_list[2], ROW_BLOCKS, COL_BLOCKS, KEPT, 0)
    left_gram = draw_left_gram(jax.random.fold_in(key_list[8], 71), 0)
    right_gram = draw_right_gram(jax.random.fold_in(key_list[8], 71), 0)
    left_basis = gaussian(key_list[5], (SEQ_SHARDS, DP_SHARDS, OWNED, BLOCK, BLOCK), BLOCK ** -0.5, 0.75, ((0, 8), (1, 64)), jnp.float32)
    right_basis = gaussian(key_list[6], (SEQ_SHARDS, DP_SHARDS, OWNED, BLOCK, BLOCK), BLOCK ** -0.5, 0.75, ((0, 8), (1, 64)), jnp.float32)
    second_moment = jnp.clip(jnp.exp(math.log(0.04) - 2.30258502 * jax.random.uniform(key_list[7], (SEQ_SHARDS, DP_SHARDS, OWNED, BLOCK, BLOCK), jnp.float32) ** levels(key_list[7], (SEQ_SHARDS, DP_SHARDS, OWNED, BLOCK, BLOCK), ((0, 8), (1, 64)), -0.2, 0.2)), 0.004, 0.04)
    return {"acts": acts, "upstream": upstream, "keep_lists": keep_lists, "left_gram": left_gram, "right_gram": right_gram, "left_basis": left_basis, "right_basis": right_basis, "second_moment": second_moment}


def precondition(gradient, left_gram, right_gram, left_basis, right_basis, second_moment):
    highest = lax.Precision.HIGHEST
    new_left = 0.95 * left_gram + 0.05 * jnp.einsum('...ij,...kj->...ik', gradient, gradient, precision=highest)
    new_right = 0.95 * right_gram + 0.05 * jnp.einsum('...ji,...jk->...ik', gradient, gradient, precision=highest)
    partial_rot = jnp.einsum('...ji,...jk->...ik', left_basis, gradient, precision=highest)
    rotated = jnp.einsum('...ij,...jk->...ik', partial_rot, right_basis, precision=highest)
    second = 0.95 * second_moment + 0.05 * rotated * rotated
    scaled = rotated / (jnp.sqrt(second) + 1e-08)
    partial_back = jnp.einsum('...ij,...jk->...ik', left_basis, scaled, precision=highest)
    direction = jnp.einsum('...ij,...kj->...ik', partial_back, right_basis, precision=highest)
    return (new_left, new_right, direction)

def reference(acts, upstream, keep_lists, left_gram, right_gram, left_basis, right_basis, second_moment):
    grad = jnp.dot(acts.T, upstream, preferred_element_type=jnp.float32)
    tiles = grad.reshape(ROW_BLOCKS, BLOCK, COL_BLOCKS, BLOCK)
    picked = jnp.take_along_axis(tiles, keep_lists.astype(jnp.int32)[:, None, :, None], axis=2)
    blocks = picked.transpose(0, 2, 1, 3).reshape(SEQ_SHARDS, DP_SHARDS, OWNED, BLOCK, BLOCK)
    new_left, new_right, direction = precondition(blocks, left_gram, right_gram, left_basis, right_basis, second_moment)
    return (new_left, new_right, direction)
```

```python
import jax
import jax.numpy as jnp
from jax import lax
from jax.experimental import pallas as pl
from jax.experimental.pallas import tpu as pltpu
from jax.sharding import Mesh, PartitionSpec as P

BLOCK = 64
HALF = BLOCK // 2
LANES = 128
DATA = ("zh", "zl", "x")
SEQ = ("y", "c")
HIGHEST = lax.Precision.HIGHEST


def grad_kernel(keep_ref, acts_ref, own_ref, other_ref, out_ref, tiles_ref):
    core = lax.axis_index("c")
    seq = lax.axis_index("y") * lax.axis_size("c") + core
    rows = acts_ref.shape[2] * acts_ref.shape[0]
    feats = acts_ref.shape[3]
    share_blocks = feats // BLOCK
    acts_own = acts_ref[:, core].reshape(rows, feats)
    acts_other = acts_ref[:, 1 - core].reshape(rows, feats)
    dims = (((0,), (0,)), ((), ()))
    for n in range(own_ref.shape[1] // 256):
        cols = slice(n * 256, n * 256 + 256)
        part = lax.dot_general(acts_own, own_ref[:, cols], dims, preferred_element_type=jnp.float32)
        part += lax.dot_general(
            acts_other, other_ref[:, cols], dims, preferred_element_type=jnp.float32
        )
        tiles_ref[2 * n] = part[:, :LANES]
        tiles_ref[2 * n + 1] = part[:, LANES:]
    left = lax.broadcasted_iota(jnp.int32, (HALF, LANES), 1) < BLOCK
    for r in range(share_blocks):
        for k in range(keep_ref.shape[0]):
            col = keep_ref[k, seq * share_blocks + r]
            tile = col // 2
            odd = (col % 2) == 1
            top = tiles_ref[tile, r * BLOCK : r * BLOCK + HALF, :]
            low = tiles_ref[tile, r * BLOCK + HALF : (r + 1) * BLOCK, :]
            top_side = jnp.where(odd, pltpu.roll(top, BLOCK, 1), top)
            low_side = jnp.where(odd, low, pltpu.roll(low, BLOCK, 1))
            out_ref[k, r * HALF : (r + 1) * HALF, :] = jnp.where(left, top_side, low_side)


def kept_partials(keep, acts, own, other):
    kept = keep.shape[0]
    feats = acts.shape[-1]
    return pl.pallas_call(
        grad_kernel,
        out_shape=jax.ShapeDtypeStruct((kept, feats // 2, LANES), jnp.float32),
        in_specs=[pl.BlockSpec(memory_space=pltpu.SMEM)]
        + [pl.BlockSpec(memory_space=pltpu.VMEM)] * 3,
        out_specs=pl.BlockSpec(memory_space=pltpu.VMEM),
        scratch_shapes=[pltpu.VMEM((own.shape[1] // LANES, feats, LANES), jnp.float32)],
        name="kept_partials",
    )(keep, acts, own, other)


def dot(a, b, ca, cb):
    return lax.dot_general(
        a, b, (((ca,), (cb,)), ((), ())), precision=HIGHEST, preferred_element_type=jnp.float32
    )


def step_kernel(parts_ref, lg_ref, rg_ref, lb_ref, rb_ref, sm_ref, nl_ref, nr_ref, dir_ref):
    packed = jnp.sum(parts_ref[...], axis=0)
    g = jnp.concatenate([packed[:, :BLOCK], packed[:, BLOCK:]], axis=0)
    lb = lb_ref[...]
    rb = rb_ref[...]
    rotated = dot(dot(lb, g, 0, 0), rb, 1, 0)
    second = 0.95 * sm_ref[...] + 0.05 * rotated * rotated
    scaled = rotated / (jnp.sqrt(second) + 1e-08)
    dir_ref[...] = dot(dot(lb, scaled, 1, 0), rb, 1, 1)
    nl_ref[...] = 0.95 * lg_ref[...] + 0.05 * dot(g, g, 1, 1)
    nr_ref[...] = 0.95 * rg_ref[...] + 0.05 * dot(g, g, 0, 0)


def soap_step(parts, *state):
    block = jax.ShapeDtypeStruct((BLOCK, BLOCK), jnp.float32)
    return pl.pallas_call(
        step_kernel,
        out_shape=(block, block, block),
        in_specs=[pl.BlockSpec(memory_space=pltpu.VMEM)] * 6,
        out_specs=[pl.BlockSpec(memory_space=pltpu.VMEM)] * 3,
        name="soap_step",
    )(parts, *state)


def per_device(acts, upstream, keep_lists, *state):
    tokens, cols = upstream.shape
    ny = lax.axis_size("y")
    spread = jnp.broadcast_to(upstream[None], (ny, tokens, cols))
    own = lax.all_to_all(spread, "y", split_axis=0, concat_axis=0, tiled=True)
    own = own.reshape(ny * tokens, cols)
    other = lax.ppermute(own, "c", [(0, 1), (1, 0)])
    packed = kept_partials(
        keep_lists.T, acts.reshape(ny, 2, tokens, acts.shape[1]), own, other
    )
    near = lax.all_to_all(packed, ("zl", "x"), split_axis=0, concat_axis=0, tiled=True)
    summed = jnp.sum(near, axis=0).reshape(-1, HALF, LANES)
    parts = lax.all_to_all(summed, "zh", split_axis=0, concat_axis=0, tiled=True)
    shape = state[0].shape
    outs = soap_step(parts, *[s.reshape(BLOCK, BLOCK) for s in state])
    return tuple(o.reshape(shape) for o in outs)


def solution(mesh):
    fine = Mesh(mesh.devices.reshape(8, 2, 4, 4, 2), DATA + SEQ)
    state = P(SEQ, DATA, None, None, None)
    in_specs = (P(DATA, SEQ), P(DATA + SEQ, None), P()) + (state,) * 5
    return jax.shard_map(
        per_device, mesh=fine, in_specs=in_specs, out_specs=(state,) * 3, check_vma=False
    )
```

```python
import jax
import jax.numpy as jnp
from jax import lax
from jax.experimental import pallas as pl
from jax.experimental.pallas import tpu as pltpu
from jax.sharding import Mesh, PartitionSpec as P

BLOCK = 64
HALF = BLOCK // 2
LANES = 128
DATA = ("zh", "zl", "x")
SEQ = ("y", "c")
SCALE = 1024.0
HIGHEST = lax.Precision.HIGHEST


def pack_kernel(keep_ref, grad_ref, out_ref):
    seq = lax.axis_index("y") * lax.axis_size("c") + lax.axis_index("c")
    share_blocks = grad_ref.shape[0] // BLOCK
    left = lax.broadcasted_iota(jnp.int32, (HALF, LANES), 1) < BLOCK
    for r in range(share_blocks):
        for k in range(keep_ref.shape[0]):
            col = keep_ref[k, seq * share_blocks + r]
            lanes = pl.ds(pl.multiple_of((col // 2) * LANES, LANES), LANES)
            odd = (col % 2) == 1
            top = grad_ref[r * BLOCK : r * BLOCK + HALF, lanes]
            low = grad_ref[r * BLOCK + HALF : (r + 1) * BLOCK, lanes]
            top_side = jnp.where(odd, pltpu.roll(top, BLOCK, 1), top)
            low_side = jnp.where(odd, low, pltpu.roll(low, BLOCK, 1))
            out_ref[k, r * HALF : (r + 1) * HALF, :] = jnp.where(left, top_side, low_side)


def pin(x):
    return pltpu.with_memory_space_constraint(x, pltpu.VMEM)


def pack_kept(keep, grad):
    kept = keep.shape[0]
    return pl.pallas_call(
        pack_kernel,
        out_shape=pltpu.VMEM((kept, grad.shape[0] // 2, LANES), jnp.float32),
        in_specs=[
            pl.BlockSpec(memory_space=pltpu.SMEM),
            pl.BlockSpec(memory_space=pltpu.VMEM),
        ],
        out_specs=pl.BlockSpec(memory_space=pltpu.VMEM),
        name="pack_kept",
    )(keep, pin(grad))


def dot(a, b, ca, cb):
    return lax.dot_general(
        a, b, (((ca,), (cb,)), ((), ())), precision=HIGHEST, preferred_element_type=jnp.float32
    )


def step_kernel(parts_ref, lg_ref, rg_ref, lb_ref, rb_ref, sm_ref, nl_ref, nr_ref, dir_ref):
    packed = jnp.sum(parts_ref[...], axis=0) * (1.0 / SCALE)
    g = jnp.concatenate([packed[:, :BLOCK], packed[:, BLOCK:]], axis=0)
    lb = lb_ref[...]
    rb = rb_ref[...]
    rotated = dot(dot(lb, g, 0, 0), rb, 1, 0)
    second = 0.95 * sm_ref[...] + 0.05 * rotated * rotated
    scaled = rotated / (jnp.sqrt(second) + 1e-08)
    dir_ref[...] = dot(dot(lb, scaled, 1, 0), rb, 1, 1)
    nl_ref[...] = 0.95 * lg_ref[...] + 0.05 * dot(g, g, 1, 1)
    nr_ref[...] = 0.95 * rg_ref[...] + 0.05 * dot(g, g, 0, 0)


def soap_step(parts, *state):
    out = jax.ShapeDtypeStruct((BLOCK, BLOCK), jnp.float32)
    return pl.pallas_call(
        step_kernel,
        out_shape=(out, out, out),
        in_specs=[pl.BlockSpec(memory_space=pltpu.VMEM)] * 6,
        out_specs=[pl.BlockSpec(memory_space=pltpu.VMEM)] * 3,
        name="soap_step",
    )(pin(parts), *[pin(s) for s in state])


def exchange(x, axes):
    return lax.all_to_all(x, axes, split_axis=0, concat_axis=0, tiled=True)


def per_device(acts, upstream, keep_lists, *state):
    tokens, cols = upstream.shape
    ny = lax.axis_size("y")
    spread = jnp.broadcast_to(upstream[None], (ny, tokens, cols))
    own = exchange(spread, "y")
    own = own.reshape(ny * tokens, cols)
    other = lax.ppermute(own, "c", [(0, 1), (1, 0)])
    mine = lax.axis_index("c")
    feats = acts.shape[1]
    halves = acts.reshape(ny, 2, tokens, feats)

    def term(core, rows):
        half = lax.dynamic_index_in_dim(halves, core, 1, keepdims=False)
        return lax.dot_general(
            half.reshape(ny * tokens, feats),
            rows,
            (((0,), (0,)), ((), ())),
            preferred_element_type=jnp.float32,
        )

    grad = term(mine, own) + term(1 - mine, other)
    packed = pack_kept(keep_lists.T, grad)
    near = exchange((packed * SCALE).astype(jnp.float16), ("zl", "x"))
    summed = jnp.sum(near.astype(jnp.float32), axis=0).reshape(-1, HALF, LANES)
    parts = exchange(summed, "zh")
    shape = state[0].shape
    outs = soap_step(parts, *[s.reshape(BLOCK, BLOCK) for s in state])
    return tuple(o.reshape(shape) for o in outs)


def solution(mesh):
    fine = Mesh(mesh.devices.reshape(8, 2, 4, 4, 2), DATA + SEQ)
    state = P(SEQ, DATA, None, None, None)
    in_specs = (P(DATA, SEQ), P(DATA + SEQ, None), P()) + (state,) * 5
    return jax.shard_map(
        per_device, mesh=fine, in_specs=in_specs, out_specs=(state,) * 3, check_vma=False
    )
```

```python
import jax
import jax.numpy as jnp
from jax import lax
from jax.experimental import pallas as pl
from jax.experimental.pallas import tpu as pltpu
from jax.sharding import Mesh, PartitionSpec as P

BLOCK = 64
HALF = BLOCK // 2
LANES = 128
DATA = ("zh", "zl", "x")
SEQ = ("y", "c")
SCALE = 1024.0
PRECISION = lax.Precision.HIGH


def pack_kernel(keep_ref, grad_ref, out_ref):
    seq = lax.axis_index("y") * lax.axis_size("c") + lax.axis_index("c")
    share_blocks = grad_ref.shape[0] // BLOCK
    left = lax.broadcasted_iota(jnp.int32, (HALF, LANES), 1) < BLOCK
    keep = keep_ref[...]
    coded = keep << (4 * lax.broadcasted_iota(jnp.int32, keep.shape, 0))
    block = lax.broadcasted_iota(jnp.int32, keep.shape, 1) - seq * share_blocks
    codes = [jnp.sum(jnp.where(block == r, coded, 0)) for r in range(share_blocks)]
    for r, code in enumerate(codes):
        for k in range(keep_ref.shape[0]):
            col = (code >> (4 * k)) & 15
            lanes = pl.ds(pl.multiple_of((col // 2) * LANES, LANES), LANES)
            odd = (col % 2) == 1
            top = grad_ref[r * BLOCK : r * BLOCK + HALF, lanes]
            low = grad_ref[r * BLOCK + HALF : (r + 1) * BLOCK, lanes]
            top_side = jnp.where(odd, pltpu.roll(top, BLOCK, 1), top)
            low_side = jnp.where(odd, low, pltpu.roll(low, BLOCK, 1))
            out_ref[k, r * HALF : (r + 1) * HALF, :] = jnp.where(left, top_side, low_side)


def pin(x):
    return pltpu.with_memory_space_constraint(x, pltpu.VMEM)


def pack_kept(keep, grad):
    kept = keep.shape[0]
    return pl.pallas_call(
        pack_kernel,
        out_shape=pltpu.VMEM((kept, grad.shape[0] // 2, LANES), jnp.float32),
        in_specs=[pl.BlockSpec(memory_space=pltpu.VMEM)] * 2,
        out_specs=pl.BlockSpec(memory_space=pltpu.VMEM),
        name="pack_kept",
    )(pin(keep), pin(grad))


def dot(a, b, ca, cb):
    return lax.dot_general(
        a, b, (((ca,), (cb,)), ((), ())), precision=PRECISION, preferred_element_type=jnp.float32
    )


def step_kernel(parts_ref, lg_ref, rg_ref, lb_ref, rb_ref, sm_ref, nl_ref, nr_ref, dir_ref):
    packed = jnp.sum(parts_ref[...], axis=0) * (1.0 / SCALE)
    g = jnp.concatenate([packed[:, :BLOCK], packed[:, BLOCK:]], axis=0)
    lb = lb_ref[...]
    rb = rb_ref[...]
    rotated = dot(dot(lb, g, 0, 0), rb, 1, 0)
    second = 0.95 * sm_ref[...] + 0.05 * rotated * rotated
    scaled = rotated / (jnp.sqrt(second) + 1e-08)
    dir_ref[...] = dot(dot(lb, scaled, 1, 0), rb, 1, 1)
    nl_ref[...] = 0.95 * lg_ref[...] + 0.05 * dot(g, g, 1, 1)
    nr_ref[...] = 0.95 * rg_ref[...] + 0.05 * dot(g, g, 0, 0)


def soap_step(parts, *state):
    out = jax.ShapeDtypeStruct((BLOCK, BLOCK), jnp.float32)
    return pl.pallas_call(
        step_kernel,
        out_shape=(out, out, out),
        in_specs=[pl.BlockSpec(memory_space=pltpu.VMEM)] * 6,
        out_specs=[pl.BlockSpec(memory_space=pltpu.VMEM)] * 3,
        name="soap_step",
    )(pin(parts), *[pin(s) for s in state])


def exchange(x, axes):
    return lax.all_to_all(x, axes, split_axis=0, concat_axis=0, tiled=True)


def per_device(acts, upstream, keep_lists, *state):
    tokens, cols = upstream.shape
    ny = lax.axis_size("y")
    spread = jnp.broadcast_to(upstream[None], (ny, tokens, cols))
    own = exchange(spread, "y")
    own = own.reshape(ny * tokens, cols)
    other = lax.ppermute(own, "c", [(0, 1), (1, 0)])
    mine = lax.axis_index("c")
    feats = acts.shape[1]
    halves = acts.reshape(ny, 2, tokens, feats)

    def term(core, rows):
        half = lax.dynamic_index_in_dim(halves, core, 1, keepdims=False)
        return lax.dot_general(
            half.reshape(ny * tokens, feats),
            rows,
            (((0,), (0,)), ((), ())),
            preferred_element_type=jnp.float32,
        )

    grad = term(mine, own) + term(1 - mine, other)
    packed = pack_kept(keep_lists.T, grad)
    near = exchange((packed * SCALE).astype(jnp.float16), ("zl", "x"))
    summed = jnp.sum(near.astype(jnp.float32), axis=0).reshape(-1, HALF, LANES)
    parts = exchange(summed, "zh")
    shape = state[0].shape
    outs = soap_step(parts, *[s.reshape(BLOCK, BLOCK) for s in state])
    return tuple(o.reshape(shape) for o in outs)


def solution(mesh):
    fine = Mesh(mesh.devices.reshape(8, 2, 4, 4, 2), DATA + SEQ)
    state = P(SEQ, DATA, None, None, None)
    in_specs = (P(DATA, SEQ), P(DATA + SEQ, None), P()) + (state,) * 5
    return jax.shard_map(
        per_device, mesh=fine, in_specs=in_specs, out_specs=(state,) * 3, check_vma=False
    )
```

```python
import jax
import jax.numpy as jnp
from jax import lax
from jax.experimental import pallas as pl
from jax.experimental.pallas import tpu as pltpu
from jax.sharding import Mesh, PartitionSpec as P

BLOCK = 64
HALF = BLOCK // 2
LANES = 128
DATA = ("zh", "zl", "x")
SEQ = ("y", "c")
SCALE = 1024.0
FAR_ORDER = (0, 4, 2, 6, 1, 5, 3, 7)
PRECISION = lax.Precision.HIGH


def pack_kernel(keep_ref, grad_ref, out_ref):
    seq = lax.axis_index("y") * lax.axis_size("c") + lax.axis_index("c")
    share_blocks = grad_ref.shape[0] // BLOCK
    left = lax.broadcasted_iota(jnp.int32, (HALF, LANES), 1) < BLOCK
    keep = keep_ref[...]
    coded = keep << (4 * lax.broadcasted_iota(jnp.int32, keep.shape, 0))
    block = lax.broadcasted_iota(jnp.int32, keep.shape, 1) - seq * share_blocks
    codes = [jnp.sum(jnp.where(block == r, coded, 0)) for r in range(share_blocks)]
    for r, code in enumerate(codes):
        for k in range(keep_ref.shape[0]):
            col = (code >> (4 * k)) & 15
            lanes = pl.ds(pl.multiple_of((col // 2) * LANES, LANES), LANES)
            odd = (col % 2) == 1
            top = grad_ref[r * BLOCK : r * BLOCK + HALF, lanes]
            low = grad_ref[r * BLOCK + HALF : (r + 1) * BLOCK, lanes]
            top_side = jnp.where(odd, pltpu.roll(top, BLOCK, 1), top)
            low_side = jnp.where(odd, low, pltpu.roll(low, BLOCK, 1))
            spot = FAR_ORDER.index(r) * HALF
            out_ref[k, spot : spot + HALF, :] = jnp.where(left, top_side, low_side)


def pin(x):
    return pltpu.with_memory_space_constraint(x, pltpu.VMEM)


def pack_kept(keep, grad):
    kept = keep.shape[0]
    return pl.pallas_call(
        pack_kernel,
        out_shape=pltpu.VMEM((kept, grad.shape[0] // 2, LANES), jnp.float32),
        in_specs=[pl.BlockSpec(memory_space=pltpu.VMEM)] * 2,
        out_specs=pl.BlockSpec(memory_space=pltpu.VMEM),
        name="pack_kept",
    )(pin(keep), pin(grad))


def dot(a, b, ca, cb):
    return lax.dot_general(
        a, b, (((ca,), (cb,)), ((), ())), precision=PRECISION, preferred_element_type=jnp.float32
    )


def step_kernel(parts_ref, lg_ref, rg_ref, lb_ref, rb_ref, sm_ref, nl_ref, nr_ref, dir_ref):
    packed = jnp.sum(parts_ref[...], axis=0) * (1.0 / SCALE)
    g = jnp.concatenate([packed[:, :BLOCK], packed[:, BLOCK:]], axis=0)
    lb = lb_ref[...]
    rb = rb_ref[...]
    rotated = dot(dot(lb, g, 0, 0), rb, 1, 0)
    second = 0.95 * sm_ref[...] + 0.05 * rotated * rotated
    scaled = rotated / (jnp.sqrt(second) + 1e-08)
    dir_ref[...] = dot(dot(lb, scaled, 1, 0), rb, 1, 1)
    nl_ref[...] = 0.95 * lg_ref[...] + 0.05 * dot(g, g, 1, 1)
    nr_ref[...] = 0.95 * rg_ref[...] + 0.05 * dot(g, g, 0, 0)


def soap_step(parts, *state):
    out = jax.ShapeDtypeStruct((BLOCK, BLOCK), jnp.float32)
    return pl.pallas_call(
        step_kernel,
        out_shape=(out, out, out),
        in_specs=[pl.BlockSpec(memory_space=pltpu.VMEM)] * 6,
        out_specs=[pl.BlockSpec(memory_space=pltpu.VMEM)] * 3,
        name="soap_step",
    )(pin(parts), *[pin(s) for s in state])


def exchange(x, axes, order=None):
    groups = None if order is None else [list(order)]
    return lax.all_to_all(
        x, axes, split_axis=0, concat_axis=0, tiled=True, axis_index_groups=groups
    )


def per_device(acts, upstream, keep_lists, *state):
    tokens, cols = upstream.shape
    ny = lax.axis_size("y")
    spread = jnp.broadcast_to(upstream[None], (ny, tokens, cols))
    own = exchange(spread, "y")
    own = own.reshape(ny * tokens, cols)
    other = lax.ppermute(own, "c", [(0, 1), (1, 0)])
    mine = lax.axis_index("c")
    feats = acts.shape[1]
    halves = acts.reshape(ny, 2, tokens, feats)

    def term(core, rows):
        half = lax.dynamic_index_in_dim(halves, core, 1, keepdims=False)
        return lax.dot_general(
            half.reshape(ny * tokens, feats),
            rows,
            (((0,), (0,)), ((), ())),
            preferred_element_type=jnp.float32,
        )

    grad = term(mine, own) + term(1 - mine, other)
    packed = pack_kept(keep_lists.T, grad)
    near = exchange((packed * SCALE).astype(jnp.float16), ("zl", "x"))
    summed = jnp.sum(near.astype(jnp.float32), axis=0).reshape(-1, HALF, LANES)
    parts = exchange(summed, "zh", FAR_ORDER)
    shape = state[0].shape
    outs = soap_step(parts, *[s.reshape(BLOCK, BLOCK) for s in state])
    return tuple(o.reshape(shape) for o in outs)


def solution(mesh):
    fine = Mesh(mesh.devices.reshape(8, 2, 4, 4, 2), DATA + SEQ)
    state = P(SEQ, DATA, None, None, None)
    in_specs = (P(DATA, SEQ), P(DATA + SEQ, None), P()) + (state,) * 5
    return jax.shard_map(
        per_device, mesh=fine, in_specs=in_specs, out_specs=(state,) * 3, check_vma=False
    )
```

```python
import jax
import jax.numpy as jnp
from jax import lax
from jax.experimental import pallas as pl
from jax.experimental.pallas import tpu as pltpu
from jax.sharding import Mesh, PartitionSpec as P

BLOCK = 64
HALF = BLOCK // 2
LANES = 128
DATA = ("zh", "zl", "x")
SEQ = ("y", "c")
SCALE = 1024.0
FAR_ORDER = (0, 4, 2, 6, 1, 5, 3, 7)
PRECISION = lax.Precision.HIGH


def pack_kernel(keep_ref, grad_ref, out_ref):
    share_blocks = grad_ref.shape[0] // BLOCK
    left = lax.broadcasted_iota(jnp.int32, (HALF, LANES), 1) < BLOCK
    for r in range(share_blocks):
        for k in range(keep_ref.shape[0]):
            col = keep_ref[k, r]
            lanes = pl.ds(pl.multiple_of((col // 2) * LANES, LANES), LANES)
            odd = (col % 2) == 1
            top = grad_ref[r * BLOCK : r * BLOCK + HALF, lanes]
            low = grad_ref[r * BLOCK + HALF : (r + 1) * BLOCK, lanes]
            top_side = jnp.where(odd, pltpu.roll(top, BLOCK, 1), top)
            low_side = jnp.where(odd, low, pltpu.roll(low, BLOCK, 1))
            spot = FAR_ORDER.index(r) * HALF
            out_ref[k, spot : spot + HALF, :] = jnp.where(left, top_side, low_side)


def pin(x):
    return pltpu.with_memory_space_constraint(x, pltpu.VMEM)


def share_kernel(keep_ref, out_ref):
    seq = lax.axis_index("y") * lax.axis_size("c") + lax.axis_index("c")
    for k in range(out_ref.shape[0]):
        for r in range(out_ref.shape[1]):
            out_ref[k, r] = keep_ref[k, seq * out_ref.shape[1] + r]


def kept_share(keep, share_blocks):
    return pl.pallas_call(
        share_kernel,
        out_shape=pltpu.SMEM((keep.shape[0], share_blocks), keep.dtype),
        in_specs=[pl.BlockSpec(memory_space=pltpu.SMEM)],
        out_specs=pl.BlockSpec(memory_space=pltpu.SMEM),
        name="kept_share",
    )(keep)


def pack_kept(keep, grad):
    kept = keep.shape[0]
    return pl.pallas_call(
        pack_kernel,
        out_shape=pltpu.VMEM((kept, grad.shape[0] // 2, LANES), jnp.float32),
        in_specs=[
            pl.BlockSpec(memory_space=pltpu.SMEM),
            pl.BlockSpec(memory_space=pltpu.VMEM),
        ],
        out_specs=pl.BlockSpec(memory_space=pltpu.VMEM),
        name="pack_kept",
    )(pltpu.with_memory_space_constraint(keep, pltpu.SMEM), pin(grad))


def dot(a, b, ca, cb):
    return lax.dot_general(
        a, b, (((ca,), (cb,)), ((), ())), precision=PRECISION, preferred_element_type=jnp.float32
    )


def step_kernel(parts_ref, lg_ref, rg_ref, lb_ref, rb_ref, sm_ref, nl_ref, nr_ref, dir_ref):
    packed = jnp.sum(parts_ref[...], axis=0) * (1.0 / SCALE)
    g = jnp.concatenate([packed[:, :BLOCK], packed[:, BLOCK:]], axis=0)
    lb = lb_ref[...]
    rb = rb_ref[...]
    rotated = dot(dot(lb, g, 0, 0), rb, 1, 0)
    second = 0.95 * sm_ref[...] + 0.05 * rotated * rotated
    scaled = rotated / (jnp.sqrt(second) + 1e-08)
    dir_ref[...] = dot(dot(lb, scaled, 1, 0), rb, 1, 1)
    nl_ref[...] = 0.95 * lg_ref[...] + 0.05 * dot(g, g, 1, 1)
    nr_ref[...] = 0.95 * rg_ref[...] + 0.05 * dot(g, g, 0, 0)


def soap_step(parts, *state):
    out = jax.ShapeDtypeStruct((BLOCK, BLOCK), jnp.float32)
    return pl.pallas_call(
        step_kernel,
        out_shape=(out, out, out),
        in_specs=[pl.BlockSpec(memory_space=pltpu.VMEM)] * 6,
        out_specs=[pl.BlockSpec(memory_space=pltpu.VMEM)] * 3,
        name="soap_step",
    )(pin(parts), *[pin(s) for s in state])


def exchange(x, axes, order=None):
    groups = None if order is None else [list(order)]
    return lax.all_to_all(
        x, axes, split_axis=0, concat_axis=0, tiled=True, axis_index_groups=groups
    )


def per_device(acts, upstream, keep_lists, *state):
    tokens, cols = upstream.shape
    ny = lax.axis_size("y")
    spread = jnp.broadcast_to(upstream[None], (ny, tokens, cols))
    own = exchange(spread, "y")
    own = own.reshape(ny * tokens, cols)
    other = lax.ppermute(own, "c", [(0, 1), (1, 0)])
    mine = lax.axis_index("c")
    feats = acts.shape[1]
    halves = acts.reshape(ny, 2, tokens, feats)

    def term(core, rows):
        half = lax.dynamic_index_in_dim(halves, core, 1, keepdims=False)
        return lax.dot_general(
            half.reshape(ny * tokens, feats),
            rows,
            (((0,), (0,)), ((), ())),
            preferred_element_type=jnp.float32,
        )

    grad = term(mine, own) + term(1 - mine, other)
    packed = pack_kept(kept_share(keep_lists.T, acts.shape[1] // BLOCK), grad)
    near = exchange((packed * SCALE).astype(jnp.float16), ("zl", "x"))
    summed = jnp.sum(near.astype(jnp.float32), axis=0).reshape(-1, HALF, LANES)
    parts = exchange(summed, "zh", FAR_ORDER)
    shape = state[0].shape
    outs = soap_step(parts, *[s.reshape(BLOCK, BLOCK) for s in state])
    return tuple(o.reshape(shape) for o in outs)


def solution(mesh):
    fine = Mesh(mesh.devices.reshape(8, 2, 4, 4, 2), DATA + SEQ)
    state = P(SEQ, DATA, None, None, None)
    in_specs = (P(DATA, SEQ), P(DATA + SEQ, None), P()) + (state,) * 5
    return jax.shard_map(
        per_device, mesh=fine, in_specs=in_specs, out_specs=(state,) * 3, check_vma=False
    )
```

```python
import jax
import jax.numpy as jnp
from jax import lax
from jax.experimental import pallas as pl
from jax.experimental.pallas import tpu as pltpu
from jax.sharding import Mesh, PartitionSpec as P

BLOCK = 64
HALF = BLOCK // 2
LANES = 128
DATA = ("zh", "zl", "x")
SEQ = ("y", "c")
SCALE = 1024.0
RING_ORDER = (0, 1, 3, 2)
FAR_ORDER = (0, 4, 2, 6, 1, 5, 3, 7)
PRECISION = lax.Precision.HIGH


def pack_kernel(keep_ref, grad_ref, out_ref):
    share_blocks = grad_ref.shape[0] // BLOCK
    left = lax.broadcasted_iota(jnp.int32, (HALF, LANES), 1) < BLOCK
    for r in range(share_blocks):
        for k in range(keep_ref.shape[0]):
            col = keep_ref[k, r]
            lanes = pl.ds(pl.multiple_of((col // 2) * LANES, LANES), LANES)
            odd = (col % 2) == 1
            top = grad_ref[r * BLOCK : r * BLOCK + HALF, lanes]
            low = grad_ref[r * BLOCK + HALF : (r + 1) * BLOCK, lanes]
            top_side = jnp.where(odd, pltpu.roll(top, BLOCK, 1), top)
            low_side = jnp.where(odd, low, pltpu.roll(low, BLOCK, 1))
            spot = FAR_ORDER.index(r) * HALF
            out_ref[k, spot : spot + HALF, :] = jnp.where(left, top_side, low_side)


def pin(x):
    return pltpu.with_memory_space_constraint(x, pltpu.VMEM)


def share_kernel(keep_ref, out_ref):
    seq = lax.axis_index("y") * lax.axis_size("c") + lax.axis_index("c")
    for k in range(out_ref.shape[0]):
        for r in range(out_ref.shape[1]):
            out_ref[k, r] = keep_ref[k, seq * out_ref.shape[1] + r]


def kept_share(keep, share_blocks):
    return pl.pallas_call(
        share_kernel,
        out_shape=pltpu.SMEM((keep.shape[0], share_blocks), keep.dtype),
        in_specs=[pl.BlockSpec(memory_space=pltpu.SMEM)],
        out_specs=pl.BlockSpec(memory_space=pltpu.SMEM),
        name="kept_share",
    )(keep)


def pack_kept(keep, grad):
    kept = keep.shape[0]
    return pl.pallas_call(
        pack_kernel,
        out_shape=pltpu.VMEM((kept, grad.shape[0] // 2, LANES), jnp.float32),
        in_specs=[
            pl.BlockSpec(memory_space=pltpu.SMEM),
            pl.BlockSpec(memory_space=pltpu.VMEM),
        ],
        out_specs=pl.BlockSpec(memory_space=pltpu.VMEM),
        name="pack_kept",
    )(pltpu.with_memory_space_constraint(keep, pltpu.SMEM), pin(grad))


def dot(a, b, ca, cb):
    return lax.dot_general(
        a, b, (((ca,), (cb,)), ((), ())), precision=PRECISION, preferred_element_type=jnp.float32
    )


def step_kernel(parts_ref, lg_ref, rg_ref, lb_ref, rb_ref, sm_ref, nl_ref, nr_ref, dir_ref):
    packed = jnp.sum(parts_ref[...], axis=0) * (1.0 / SCALE)
    g = jnp.concatenate([packed[:, :BLOCK], packed[:, BLOCK:]], axis=0)
    lb = lb_ref[...]
    rb = rb_ref[...]
    rotated = dot(dot(lb, g, 0, 0), rb, 1, 0)
    second = 0.95 * sm_ref[...] + 0.05 * rotated * rotated
    scaled = rotated / (jnp.sqrt(second) + 1e-08)
    dir_ref[...] = dot(dot(lb, scaled, 1, 0), rb, 1, 1)
    nl_ref[...] = 0.95 * lg_ref[...] + 0.05 * dot(g, g, 1, 1)
    nr_ref[...] = 0.95 * rg_ref[...] + 0.05 * dot(g, g, 0, 0)


def soap_step(parts, *state):
    out = jax.ShapeDtypeStruct((BLOCK, BLOCK), jnp.float32)
    return pl.pallas_call(
        step_kernel,
        out_shape=(out, out, out),
        in_specs=[pl.BlockSpec(memory_space=pltpu.VMEM)] * 6,
        out_specs=[pl.BlockSpec(memory_space=pltpu.VMEM)] * 3,
        name="soap_step",
    )(pin(parts), *[pin(s) for s in state])


def exchange(x, axes, order=None):
    groups = None if order is None else [list(order)]
    return lax.all_to_all(
        x, axes, split_axis=0, concat_axis=0, tiled=True, axis_index_groups=groups
    )


def per_device(acts, upstream, keep_lists, *state):
    tokens, cols = upstream.shape
    ny = lax.axis_size("y")
    spread = jnp.broadcast_to(upstream[None], (ny, tokens, cols))
    own = exchange(spread, "y", RING_ORDER)
    own = own.reshape(ny * tokens, cols)
    other = lax.ppermute(own, "c", [(0, 1), (1, 0)])
    mine = lax.axis_index("c")
    feats = acts.shape[1]
    halves = acts.reshape(ny, 2, tokens, feats)
    halves = jnp.stack([halves[chip] for chip in RING_ORDER])

    def term(core, rows):
        half = lax.dynamic_index_in_dim(halves, core, 1, keepdims=False)
        return lax.dot_general(
            half.reshape(ny * tokens, feats),
            rows,
            (((0,), (0,)), ((), ())),
            preferred_element_type=jnp.float32,
        )

    grad = term(mine, own) + term(1 - mine, other)
    packed = pack_kept(kept_share(keep_lists.T, acts.shape[1] // BLOCK), grad)
    near = exchange((packed * SCALE).astype(jnp.float16), ("zl", "x"))
    summed = jnp.sum(near.astype(jnp.float32), axis=0).reshape(-1, HALF, LANES)
    parts = exchange(summed, "zh", FAR_ORDER)
    shape = state[0].shape
    outs = soap_step(parts, *[s.reshape(BLOCK, BLOCK) for s in state])
    return tuple(o.reshape(shape) for o in outs)


def solution(mesh):
    fine = Mesh(mesh.devices.reshape(8, 2, 4, 4, 2), DATA + SEQ)
    state = P(SEQ, DATA, None, None, None)
    in_specs = (P(DATA, SEQ), P(DATA + SEQ, None), P()) + (state,) * 5
    return jax.shard_map(
        per_device, mesh=fine, in_specs=in_specs, out_specs=(state,) * 3, check_vma=False
    )
```
